32 devices in a mesh: child: 2 (over y), row: 4 (over x, core), col: 4 (over z).
Axes of the slice: x: 2, y: 2, z: 4, core: 2. Of those that a mesh axis runs over, the one named last changes fastest.
Arguments:
- child_blocks: float32 [2, 4096, 4096], P('child', 'row', 'col'), as said below
- child_panels: bfloat16 [2, 4096, 1024], P('child', 'row'), may hold values from -0.1875 to 0.1875
- child_patterns: int32 [2, 16, 16], replicated, may hold values from 0 to 1, as said below
- child_maps: int32 [2, 16], replicated, may hold values from 0 to 23, as said below
- parent_place: int32 [24], replicated, may hold values from 0 to 23, as said below
- parent_front: float32 [6144, 6144], P(('child', 'row'), 'col'), as said below
Outputs:
- factored: float32 [6144, 6144], P(('child', 'row'), 'col')
The draws below stay inside these ranges and needn't reach their ends.
Inputs may be any that keep to these rules, and one draw needn't show every extreme that they name: `parent_place`: a permutation. The entries of one child are distinct; within each aligned block of 4 entries of one child, the values parent_place[child_maps[c, i]] // 6 are distinct. `child_patterns`: symmetric in its two tile dimensions, with ones on the diagonal. `child_blocks`: each child's block is symmetric. `parent_front`: symmetric; the diagonal entries inside stored tiles (parent_place[0], parent_place[0]) and (parent_place[1], parent_place[1]) lie between 200 and 400.
All inputs are finite; a program needn't handle non-finite values.
Results may differ from the reference program's by a relative error of at most 0.0003.
Values may be sent and summed in bfloat16 or wider, within the bound.
A program may use at most 128 MiB of HBM per device.

```python
import math
import jax
import jax.numpy as jnp
from jax import lax

TILE = 256
DEPTH = 1024
CHILD_TILES_DEV = 4
PARENT_TILES_DEV = 3
PANEL = 512
CHILD_TILES = 16
PARENT_TILES = 24
CHILD_ORDER = 4096
PARENT_ORDER = 6144


def move_front(within, slot_value, group_width, index_pos):
    target_group = slot_value // group_width
    target_pos = slot_value % group_width
    group_row = within[target_group]
    positions = jnp.arange(group_width)
    current = group_row[index_pos]
    new_row = jnp.where(group_row == target_pos, current, jnp.where(positions == index_pos, target_pos, group_row))
    return within.at[target_group].set(new_row)


def layout_tables(key):
    folded = jax.random.fold_in(key, 11)
    place_key, child_key = jax.random.split(folded)
    ordering = jax.random.permutation(place_key, PARENT_TILES).astype(jnp.int32)
    inverse = jnp.argsort(ordering).astype(jnp.int32)
    blocks = CHILD_TILES // CHILD_TILES_DEV
    stride = blocks // CHILD_TILES_DEV
    group_width = 2 * PARENT_TILES_DEV
    mappings = []
    for member in range(2):
        subkeys = jax.random.split(jax.random.fold_in(child_key, member), 4)
        relabel = jax.random.permutation(subkeys[0], blocks)
        block_order = jax.random.permutation(subkeys[1], blocks)
        within = jax.vmap(lambda subkey: jax.random.permutation(subkey, group_width))(jax.random.split(subkeys[2], blocks))
        within = move_front(within, ordering[PARENT_TILES - 1], group_width, 0)
        within = move_front(within, ordering[0], group_width, 1)
        position = jax.vmap(lambda subkey: jax.random.permutation(subkey, CHILD_TILES_DEV))(jax.random.split(subkeys[3], blocks))
        block_ids = jnp.arange(blocks)[:, None]
        ranks_row = jnp.arange(CHILD_TILES_DEV)[None, :]
        groups = relabel[(block_ids + ranks_row * stride) % blocks]
        slot_ids = groups * group_width + within[groups, ranks_row]
        tile_ids = block_order[block_ids] * CHILD_TILES_DEV + position
        mapping = jnp.zeros((CHILD_TILES,), jnp.int32).at[tile_ids.reshape(-1)].set(inverse[slot_ids].reshape(-1))
        mappings.append(mapping)
    return (ordering, jnp.stack(mappings).astype(jnp.int32))


def draw_parent_place(key, part):
    return layout_tables(key)[0]


def draw_child_maps(key, part):
    return layout_tables(key)[1]


def draw_child_patterns(key, part):
    folded = jax.random.fold_in(key, 23)
    first, second = jax.random.split(folded)
    density = jax.random.randint(first, (2, 1, 1), 35, 96)
    rolls = jax.random.randint(second, (2, CHILD_TILES, CHILD_TILES), 0, 100)
    lower = jnp.tril(rolls < density)
    symmetric = jnp.logical_or(lower, jnp.swapaxes(lower, 1, 2))
    identity = jnp.eye(CHILD_TILES, dtype=bool)[None]
    return jnp.where(identity, 1, symmetric.astype(jnp.int32)).astype(jnp.int32)


def draw_child_blocks(key, part):
    folded = jax.random.fold_in(key, 31)
    dims_shape = (2, CHILD_ORDER, CHILD_ORDER)
    raw_values = jax.random.normal(folded, dims_shape, jnp.float32)
    return (raw_values + jnp.swapaxes(raw_values, 1, 2)) / math.sqrt(2.0)


def draw_parent_front(key, part):
    ordering = layout_tables(key)[0]
    folded = jax.random.fold_in(key, 37)
    first, second = jax.random.split(folded)
    dims_shape = (PARENT_ORDER, PARENT_ORDER)
    raw_values = jax.random.normal(first, dims_shape, jnp.float32)
    symmetric = (raw_values + raw_values.T) / math.sqrt(2.0)
    tile_ids = jnp.arange(PARENT_ORDER) // TILE
    pivot = jnp.logical_or(tile_ids == ordering[0], tile_ids == ordering[1])
    strip = pivot[:, None] != pivot[None, :]
    scaled = jnp.where(strip, 4.0 * symmetric, symmetric)
    diagonal = jax.random.uniform(second, (PARENT_ORDER,), jnp.float32, 200.0, 400.0)
    identity = jnp.logical_and(jnp.eye(PARENT_ORDER, dtype=bool), pivot[:, None])
    return jnp.where(identity, diagonal[None, :], scaled)


def shard_levels(own_key, shape, cuts, least, largest):
    def one(dim, parts):
        draws = jax.random.uniform(jax.random.fold_in(jax.random.fold_in(own_key, 6), dim), (parts,), jnp.float32, least / len(cuts), largest / len(cuts))
        return jnp.repeat(jnp.exp(draws), shape[dim] // parts).reshape((-1,) + (1,) * (len(shape) - dim - 1))

    factor_of = one(*cuts[0])
    for cut in cuts[1:]:
        factor_of = factor_of * one(*cut)
    return factor_of


def noise(rng, shape, spread, limit, cuts=(), kind=jnp.bfloat16):
    factor_of = shard_levels(rng, shape, cuts, -0.22, 0.18) if cuts else 1.0
    values = jax.random.normal(rng, shape, jnp.float32) * spread * factor_of
    return jnp.minimum(jnp.maximum(values, -limit), limit).astype(kind)


def setup_inputs(seed: int = 0) -> dict:
    key_list = jax.random.split(jax.random.key(seed), 7)
    return {
        "child_blocks": draw_child_blocks(jax.random.fold_in(key_list[6], 71), 0),
        "child_panels": noise(key_list[1], (2, CHILD_ORDER, DEPTH), DEPTH ** -0.5, 0.1875, ((0, 2), (1, 4))),
        "child_patterns": draw_child_patterns(jax.random.fold_in(key_list[6], 71), 0),
        "child_maps": draw_child_maps(jax.random.fold_in(key_list[6], 71), 0),
        "parent_place": draw_parent_place(jax.random.fold_in(key_list[6], 71), 0),
        "parent_front": draw_parent_front(jax.random.fold_in(key_list[6], 71), 0),
    }


def reference(child_blocks, child_panels, child_patterns, child_maps, parent_place, parent_front):
    frontal = parent_front.reshape(PARENT_TILES, TILE, PARENT_TILES, TILE)
    for member in range(2):
        panel_data = child_panels[member].astype(jnp.float32)
        product = jnp.dot(panel_data.astype(jnp.float32), panel_data.T.astype(jnp.float32), precision=lax.Precision.HIGHEST, preferred_element_type=jnp.float32)
        tile_mask = child_patterns[member].astype(jnp.float32)
        update = (child_blocks[member] - product).reshape(CHILD_TILES, TILE, CHILD_TILES, TILE) * tile_mask[:, None, :, None]
        slot_list = parent_place[child_maps[member]]
        frontal = frontal.at[slot_list[:, None], :, slot_list[None, :], :].add(update.transpose(0, 2, 1, 3))
    panel_slots = parent_place[0:2]
    diagonal_block = frontal[panel_slots[:, None], :, panel_slots[None, :], :]
    diagonal_block = diagonal_block.transpose(0, 2, 1, 3).reshape(PANEL, PANEL)
    factor = jnp.linalg.cholesky(diagonal_block)
    column = frontal[:, :, panel_slots, :].reshape(PARENT_ORDER, PANEL)
    panel_rows = lax.linalg.triangular_solve(factor, column, left_side=False, lower=True, transpose_a=True)
    flattened = frontal.reshape(PARENT_ORDER, PARENT_ORDER)
    result = flattened - jnp.dot(panel_rows.astype(jnp.float32), panel_rows.T.astype(jnp.float32), precision=lax.Precision.HIGHEST, preferred_element_type=jnp.float32)
    result_tiles = result.reshape(PARENT_TILES, TILE, PARENT_TILES, TILE)
    result_tiles = result_tiles.at[:, :, panel_slots, :].set(panel_rows.reshape(PARENT_TILES, TILE, 2, TILE))
    return result_tiles.reshape(PARENT_ORDER, PARENT_ORDER)
```

```python
import functools

import jax
import jax.numpy as jnp
from jax import lax
from jax.experimental import pallas as pl
from jax.experimental.pallas import tpu as pltpu
from jax.sharding import Mesh, PartitionSpec as P

TILE = 256
F32 = jnp.float32
BF16 = jnp.bfloat16
NT = (((1,), (1,)), ((), ()))
TN = (((0,), (0,)), ((), ()))


def dot(a, b, dims):
    return lax.dot_general(a, b, dims, preferred_element_type=F32)


def split(x):
    hi = x.astype(BF16)
    return hi, (x - hi.astype(F32)).astype(BF16)


def dot3(a, b, dims):
    ah, al = split(a)
    bh, bl = split(b)
    return dot(ah, bh, dims) + (dot(ah, bl, dims) + dot(al, bh, dims))


def tile_call(kernel, grid, tables, operands, in_specs, out_shape, out_spec, name, cost=None, scratch=()):
    return pl.pallas_call(
        kernel,
        grid_spec=pltpu.PrefetchScalarGridSpec(
            num_scalar_prefetch=len(tables), grid=grid, in_specs=in_specs, out_specs=out_spec,
            scratch_shapes=list(scratch),
        ),
        out_shape=out_shape,
        name=name,
        cost_estimate=cost,
    )(*tables, *operands)


def pick_kernel(idx, loc, src, out):
    ok = loc[pl.program_id(0)] != 0
    out[0] = jnp.where(ok, src[...], jnp.zeros_like(src))


def diag_kernel(t, blk, front, ea, eb, out):
    k = pl.program_id(0) * 2 + pl.program_id(1)
    x = jnp.where(t[4, k] != 0, blk[...], 0.0) + jnp.where(t[5, k] != 0, front[...], 0.0)
    out[...] = x - jnp.where(t[6, k] != 0, dot(ea[...], eb[...], NT), 0.0)


def update_kernel(rows, fac, raw, panel, partner, out):
    f = fac[pl.program_id(0), pl.program_id(1)]
    u = raw[0] - dot(panel[...], partner[0], NT)
    out[0] = jnp.where(f != 0, u, 0.0)


def strip_kernel(t, upd, front, out):
    a, q = pl.program_id(0), pl.program_id(1)
    k = a * pl.num_programs(1) + q
    out[...] = jnp.where(t[2, k] != 0, upd[0], 0.0) + jnp.where(t[4, k] != 0, front[...], 0.0)


def final_kernel(t, front, a0, b0, a1, b1, wr, wc, out):
    k = pl.program_id(0) * pl.num_programs(1) + pl.program_id(1)
    panel = t[12, k]

    @pl.when(panel == 0)
    def _():
        x = front[...]
        for m, src in enumerate((a0, b0, a1, b1)):
            x = x + jnp.where(t[8 + m, k] != 0, src[0], 0.0)
        out[...] = x - dot3(wr[...], wc[...], TN)

    @pl.when(panel == 1)
    def _():
        out[...] = wr[:TILE, :].T

    @pl.when(panel == 2)
    def _():
        out[...] = wr[TILE:, :].T


def body(child_blocks, child_panels, child_patterns, child_maps, parent_place, parent_front):
    ci = lax.axis_index("child")
    rx = lax.axis_index("rx")
    core = lax.axis_index("core")
    col = lax.axis_index("col")
    cores = lax.axis_size("core")
    rxn = lax.axis_size("rx")
    row = rx * cores + core
    rown = rxn * cores
    chips = lax.axis_size("child") * rxn
    chip = ci * rxn + rx
    group = ci * rown + row
    block = child_blocks[0]
    own = child_panels[0]
    depth = own.shape[1]
    width = block.shape[0]
    td = width // TILE
    blocks = child_maps.shape[1] // td
    rd = parent_front.shape[0] // TILE
    cd = parent_front.shape[1] // TILE
    slots_n = parent_place.shape[0]
    i32 = jnp.int32

    slots = jnp.sum(
        jnp.where(child_maps[:, :, None] == jnp.arange(slots_n, dtype=i32), parent_place, 0), axis=2
    )
    tiles = jnp.arange(child_maps.shape[1], dtype=i32)
    hit = slots[:, None, :] == jnp.arange(slots_n, dtype=i32)[None, :, None]
    inv = jnp.sum(jnp.where(hit, tiles + 1, 0), axis=2) - 1
    mine = lax.dynamic_index_in_dim(slots, ci, 0, keepdims=False).reshape(blocks, td)
    inv_own = lax.dynamic_index_in_dim(inv, ci, 0, keepdims=False)
    pat = lax.dynamic_index_in_dim(child_patterns, ci, 0, keepdims=False)
    m = (mine // cd)[:, None, :] == jnp.arange(chips, dtype=i32)[None, :, None]
    which = jnp.sum(jnp.where(m, jnp.arange(td, dtype=i32), 0), axis=2)
    there = jnp.any(m, axis=2).astype(i32)
    row_tile = lax.dynamic_index_in_dim(which, row, 0, keepdims=False)
    row_ok = lax.dynamic_index_in_dim(there, row, 0, keepdims=False)
    out_tile = lax.dynamic_index_in_dim(which, col, 0, keepdims=False)
    out_ok = lax.dynamic_index_in_dim(there, col, 0, keepdims=False)
    in_tile = lax.dynamic_index_in_dim(which, col, 1, keepdims=False)
    in_ok = lax.dynamic_index_in_dim(there, col, 1, keepdims=False)
    e = parent_place[:2]
    ie = inv_own[e]

    outgoing = tile_call(
        pick_kernel, (blocks,), (out_tile, out_ok), (block,),
        [pl.BlockSpec((width, TILE), lambda z, i, l: (0, i[z]))],
        jax.ShapeDtypeStruct((blocks, width, TILE), F32),
        pl.BlockSpec((1, width, TILE), lambda z, i, l: (z, 0, 0)), "pick",
    )
    raw = lax.all_to_all(outgoing, "col", split_axis=0, concat_axis=0, tiled=True)

    part = lax.dynamic_slice(own, (row_tile[col] * TILE, 0), (TILE, depth))
    part = jnp.where(row_ok[col] != 0, part, jnp.zeros_like(part))

    e_here = jnp.logical_and(ie >= 0, ie // td == row)
    e_rows = jnp.concatenate([
        jnp.where(e_here[a], lax.dynamic_slice(own, ((ie[a] % td) * TILE, 0), (TILE, depth)), jnp.zeros((), BF16))
        for a in range(2)
    ])
    e_all = lax.psum(e_rows, ("rx", "core"))
    partner = lax.all_gather(part, ("rx", "core"), axis=0)
    pair_a = jnp.array([0, 0, 1, 1], i32)
    pair_b = jnp.array([0, 1, 0, 1], i32)
    ia, ib, ea, eb = ie[pair_a], ie[pair_b], e[pair_a], e[pair_b]
    live = (ia >= 0) & (ib >= 0) & (pat[jnp.maximum(ia, 0), jnp.maximum(ib, 0)] != 0)
    table = jnp.stack([
        jnp.maximum(ia, 0) % td, jnp.maximum(ib, 0) % td, ea % rd, eb % cd,
        live & (ia // td == row) & (ib // td == col),
        (ea // rd == group) & (eb // cd == col),
        live & (row == 0) & (col == 0),
    ]).astype(i32)
    diag_part = tile_call(
        diag_kernel, (2, 2), (table,), (block, parent_front, e_all, e_all),
        [
            pl.BlockSpec((TILE, TILE), lambda a, b, t: (t[0, a * 2 + b], t[1, a * 2 + b])),
            pl.BlockSpec((TILE, TILE), lambda a, b, t: (t[2, a * 2 + b], t[3, a * 2 + b])),
            pl.BlockSpec((TILE, depth), lambda a, b, t: (a, 0)),
            pl.BlockSpec((TILE, depth), lambda a, b, t: (b, 0)),
        ],
        jax.ShapeDtypeStruct((2 * TILE, 2 * TILE), F32),
        pl.BlockSpec((TILE, TILE), lambda a, b, t: (a, b)), "diag",
    )
    diagonal = lax.psum(diag_part, ("child", "rx", "core", "col"))
    factor = jnp.linalg.cholesky(diagonal)
    inverse = lax.linalg.triangular_solve(
        factor, jnp.eye(2 * TILE, dtype=F32), left_side=True, lower=True
    )

    col_ids = jnp.arange(blocks, dtype=i32) * td + in_tile
    factors = pat[row * td + row_tile][:, col_ids] * row_ok[:, None] * in_ok[None, :]
    update = tile_call(
        update_kernel, (chips, blocks), (row_tile, factors), (raw, own, partner),
        [
            pl.BlockSpec((1, TILE, TILE), lambda p, b, r, f: (b, r[p], 0)),
            pl.BlockSpec((TILE, depth), lambda p, b, r, f: (r[p], 0)),
            pl.BlockSpec((1, TILE, depth), lambda p, b, r, f: (b, 0, 0)),
        ],
        jax.ShapeDtypeStruct((chips, TILE, blocks * TILE), F32),
        pl.BlockSpec((1, TILE, TILE), lambda p, b, r, f: (p, 0, b)), "update",
    )
    first = lax.all_to_all(update, ("child", "rx"), split_axis=0, concat_axis=0, tiled=True)
    second = lax.ppermute(first, "core", [(k, (k + 1) % 2) for k in range(2)])

    my_cols = lax.dynamic_slice_in_dim(inv, col * cd, cd, 1)
    my_rows = lax.dynamic_slice_in_dim(inv, group * rd, rd, 1)
    cols_own = lax.dynamic_index_in_dim(my_cols, ci, 0, keepdims=False)
    grid_q = jnp.broadcast_to(jnp.arange(cd, dtype=i32), (2, cd))
    e2 = jnp.broadcast_to(e[:, None], (2, cd))
    cols2 = jnp.broadcast_to(cols_own[None, :], (2, cd))
    table = jnp.stack([
        e2 // cd, jnp.maximum(cols2, 0) // td,
        (e_here[:, None] & (cols2 >= 0)),
        e2 % rd, (e2 // rd == group),
    ]).astype(i32).reshape(5, 2 * cd)
    strip_part = tile_call(
        strip_kernel, (2, cd), (table,), (update, parent_front),
        [
            pl.BlockSpec((1, TILE, TILE), lambda a, q, t: (t[0, a * cd + q], 0, t[1, a * cd + q])),
            pl.BlockSpec((TILE, TILE), lambda a, q, t: (t[3, a * cd + q], q)),
        ],
        jax.ShapeDtypeStruct((2 * TILE, cd * TILE), F32),
        pl.BlockSpec((TILE, TILE), lambda a, q, t: (a, q)), "strip",
    )
    strip = lax.psum(strip_part, ("child", "rx", "core"))
    half = lax.dynamic_slice(strip, (0, core * rd * TILE), (2 * TILE, rd * TILE))
    half = lax.psum(jnp.where(chip == col, half, jnp.zeros_like(half)), "col")
    wc = lax.dot_general(inverse, strip, (((1,), (0,)), ((), ())), precision=lax.Precision.HIGHEST)
    wr = lax.dot_general(inverse, half, (((1,), (0,)), ((), ())), precision=lax.Precision.HIGHEST)

    rr = jnp.broadcast_to(my_rows[:, :, None], (2, rd, cd))
    cc = jnp.broadcast_to(my_cols[:, None, :], (2, rd, cd))
    ok = (rr >= 0) & (cc >= 0)
    send_row = jnp.maximum(rr, 0) // td
    same = send_row % cores == core
    send = jnp.arange(2, dtype=i32)[:, None, None] * rxn + send_row // cores
    from_b = jnp.maximum(cc, 0) // td
    lists = []
    for c in range(2):
        for kind in (same, ~same):
            flag = ok[c] & kind[c]
            lists.append((jnp.where(flag, send[c], 0), jnp.where(flag, from_b[c], 0), flag.astype(i32)))
    here = col * cd + jnp.arange(cd, dtype=i32)
    panel = jnp.where(here == e[0], 1, jnp.where(here == e[1], 2, 0))
    rows = [x[n] for n in (0, 1) for x in lists] + [x[2] for x in lists]
    rows.append(jnp.broadcast_to(panel, (rd, cd)))
    table = jnp.stack(rows).reshape(13, rd * cd)

    def from_list(n):
        return pl.BlockSpec(
            (1, TILE, TILE), lambda i, j, t: (t[n, i * cd + j], 0, t[4 + n, i * cd + j])
        )

    return tile_call(
        final_kernel, (rd, cd), (table,), (parent_front, first, second, first, second, wr, wc),
        [pl.BlockSpec((TILE, TILE), lambda i, j, t: (i, j))] + [from_list(n) for n in range(4)] + [
            pl.BlockSpec((2 * TILE, TILE), lambda i, j, t: (0, i)),
            pl.BlockSpec((2 * TILE, TILE), lambda i, j, t: (0, j)),
        ],
        jax.ShapeDtypeStruct(parent_front.shape, F32),
        pl.BlockSpec((TILE, TILE), lambda i, j, t: (i, j)), "final",
    )


def solution(mesh):
    child, row, col = mesh.devices.shape
    cores = child * row // col
    fine = Mesh(mesh.devices.reshape(child, row // cores, cores, col), ("child", "rx", "core", "col"))
    return jax.shard_map(
        body,
        mesh=fine,
        in_specs=(
            P("child", ("rx", "core"), "col"),
            P("child", ("rx", "core"), None),
            P(),
            P(),
            P(),
            P(("child", "rx", "core"), "col"),
        ),
        out_specs=P(("child", "rx", "core"), "col"),
        check_vma=False,
    )
```

```python
import functools

import jax
import jax.numpy as jnp
from jax import lax
from jax.experimental import pallas as pl
from jax.experimental.pallas import tpu as pltpu
from jax.sharding import Mesh, PartitionSpec as P

TILE = 256
F32 = jnp.float32
BF16 = jnp.bfloat16
NT = (((1,), (1,)), ((), ()))
TN = (((0,), (0,)), ((), ()))


def dot(a, b, dims):
    return lax.dot_general(a, b, dims, preferred_element_type=F32)


def split(x):
    hi = x.astype(BF16)
    return hi, (x - hi.astype(F32)).astype(BF16)


def dot3(a, b, dims):
    ah, al = split(a)
    bh, bl = split(b)
    return dot(ah, bh, dims) + (dot(ah, bl, dims) + dot(al, bh, dims))


def tile_call(kernel, grid, tables, operands, in_specs, out_shape, out_spec, name, cost=None, scratch=()):
    return pl.pallas_call(
        kernel,
        grid_spec=pltpu.PrefetchScalarGridSpec(
            num_scalar_prefetch=len(tables), grid=grid, in_specs=in_specs, out_specs=out_spec,
            scratch_shapes=list(scratch),
        ),
        out_shape=out_shape,
        name=name,
        cost_estimate=cost,
    )(*tables, *operands)


def pick_kernel(idx, loc, src, out):
    ok = loc[pl.program_id(0)] != 0
    out[0] = jnp.where(ok, src[...], jnp.zeros_like(src))


def diag_kernel(t, blk, front, ea, eb, out):
    k = pl.program_id(0) * 2 + pl.program_id(1)
    x = jnp.where(t[4, k] != 0, blk[...], 0.0) + jnp.where(t[5, k] != 0, front[...], 0.0)
    out[...] = x - jnp.where(t[6, k] != 0, dot(ea[...], eb[...], NT), 0.0)


def update_kernel(rows, fac, raw, panel, partner, out):
    f = fac[pl.program_id(0), pl.program_id(1)]
    u = raw[0] - dot(panel[...], partner[0], NT)
    out[0] = jnp.where(f != 0, u, 0.0)


def strip_kernel(t, upd, front, out):
    a, q = pl.program_id(0), pl.program_id(1)
    k = a * pl.num_programs(1) + q
    out[...] = jnp.where(t[2, k] != 0, upd[0], 0.0) + jnp.where(t[4, k] != 0, front[...], 0.0)


def final_kernel(t, front, a0, b0, a1, b1, wr, wc, out):
    k = pl.program_id(0) * pl.num_programs(1) + pl.program_id(1)
    panel = t[12, k]

    @pl.when(panel == 0)
    def _():
        x = front[...]
        for m, src in enumerate((a0, b0, a1, b1)):
            x = x + jnp.where(t[8 + m, k] != 0, src[0], 0.0)
        out[...] = x - dot3(wr[...], wc[...], TN)

    @pl.when(panel == 1)
    def _():
        out[...] = wr[:TILE, :].T

    @pl.when(panel == 2)
    def _():
        out[...] = wr[TILE:, :].T


BASE = 128
WIDE = 2


def base_inverse(a_ref, d_ref, x_ref):
    n, step = a_ref.shape[0], 8
    ids = lax.broadcasted_iota(jnp.int32, (step, n), 0)
    lanes = lax.broadcasted_iota(jnp.int32, (step, n), 1)
    a = [a_ref[i * step : (i + 1) * step, :] for i in range(n // step)]
    x = [(lanes == ids + i * step).astype(F32) for i in range(n // step)]
    for j in range(0, n, WIDE):
        c0 = j // step
        chunks = range(c0, n // step)
        cols = [[jnp.broadcast_to(a[i][:, j + t : j + t + 1], (step, n)) for i in chunks] for t in range(WIDE)]
        at = [j + t - c0 * step for t in range(WIDE)]
        rows = [a[c0][p : p + 1, :] for p in at]
        xrows = [x[c0][p : p + 1, :] for p in at]
        for t in range(WIDE):
            pivot = cols[t][0][at[t] : at[t] + 1, :]
            d_ref[j + t : j + t + 1, :] = pivot
            inv = 1.0 / pivot
            low = [c * inv for c in cols[t]]
            low[0] = jnp.where(ids > at[t], low[0], 0.0)
            for s in range(t + 1, WIDE):
                f = cols[t][0][at[s] : at[s] + 1, :]
                g = f * inv
                cols[s] = [c - l * f for c, l in zip(cols[s], low)]
                rows[s] = rows[s] - g * rows[t]
                xrows[s] = xrows[s] - g * xrows[t]
            for n_, i in enumerate(chunks):
                a[i] = a[i] - low[n_] * rows[t]
                x[i] = x[i] - low[n_] * xrows[t]
    for i in range(n // step):
        x_ref[i * step : (i + 1) * step, :] = x[i] * (1.0 / jnp.sqrt(d_ref[i * step : (i + 1) * step, :]))


def factor_kernel(a_in, y, a, blk, piv, inv):
    n = a.shape[0]
    high = functools.partial(lax.dot_general, precision=lax.Precision.HIGHEST, preferred_element_type=F32)
    ids = lax.broadcasted_iota(jnp.int32, (n, n), 0)
    a[...] = a_in[...]
    y[...] = (ids == lax.broadcasted_iota(jnp.int32, (n, n), 1)).astype(F32)

    def one(k, carry):
        at = pl.ds(pl.multiple_of(k * BASE, BASE), BASE)
        blk[...] = a[at, at]
        base_inverse(blk, piv, inv)
        low = high(a[:, at], inv[...], NT)
        low = jnp.where(ids[:, :BASE] >= (k + 1) * BASE, low, 0.0)
        yk = high(inv[...], y[at, :], (((1,), (0,)), ((), ())))
        a[...] = a[...] - high(low, low, NT)
        y[...] = y[...] - high(low, yk, (((1,), (0,)), ((), ())))
        y[at, :] = yk
        return carry

    lax.fori_loop(0, n // BASE, one, 0)


def factor_inverse(d):
    n = d.shape[0]
    return pl.pallas_call(
        factor_kernel,
        out_shape=jax.ShapeDtypeStruct(d.shape, F32),
        scratch_shapes=[pltpu.VMEM((n, n), F32)] + [pltpu.VMEM((BASE, BASE), F32)] * 3,
        name="factor",
    )(d)


def body(child_blocks, child_panels, child_patterns, child_maps, parent_place, parent_front):
    ci = lax.axis_index("child")
    rx = lax.axis_index("rx")
    core = lax.axis_index("core")
    col = lax.axis_index("col")
    cores = lax.axis_size("core")
    rxn = lax.axis_size("rx")
    row = rx * cores + core
    rown = rxn * cores
    chips = lax.axis_size("child") * rxn
    chip = ci * rxn + rx
    group = ci * rown + row
    block = child_blocks[0]
    own = child_panels[0]
    depth = own.shape[1]
    width = block.shape[0]
    td = width // TILE
    blocks = child_maps.shape[1] // td
    rd = parent_front.shape[0] // TILE
    cd = parent_front.shape[1] // TILE
    slots_n = parent_place.shape[0]
    i32 = jnp.int32

    slots = jnp.sum(
        jnp.where(child_maps[:, :, None] == jnp.arange(slots_n, dtype=i32), parent_place, 0), axis=2
    )
    tiles = jnp.arange(child_maps.shape[1], dtype=i32)
    hit = slots[:, None, :] == jnp.arange(slots_n, dtype=i32)[None, :, None]
    inv = jnp.sum(jnp.where(hit, tiles + 1, 0), axis=2) - 1
    mine = lax.dynamic_index_in_dim(slots, ci, 0, keepdims=False).reshape(blocks, td)
    inv_own = lax.dynamic_index_in_dim(inv, ci, 0, keepdims=False)
    pat = lax.dynamic_index_in_dim(child_patterns, ci, 0, keepdims=False)
    m = (mine // cd)[:, None, :] == jnp.arange(chips, dtype=i32)[None, :, None]
    which = jnp.sum(jnp.where(m, jnp.arange(td, dtype=i32), 0), axis=2)
    there = jnp.any(m, axis=2).astype(i32)
    row_tile = lax.dynamic_index_in_dim(which, row, 0, keepdims=False)
    row_ok = lax.dynamic_index_in_dim(there, row, 0, keepdims=False)
    out_tile = lax.dynamic_index_in_dim(which, col, 0, keepdims=False)
    out_ok = lax.dynamic_index_in_dim(there, col, 0, keepdims=False)
    in_tile = lax.dynamic_index_in_dim(which, col, 1, keepdims=False)
    in_ok = lax.dynamic_index_in_dim(there, col, 1, keepdims=False)
    e = parent_place[:2]
    ie = inv_own[e]

    outgoing = tile_call(
        pick_kernel, (blocks,), (out_tile, out_ok), (block,),
        [pl.BlockSpec((width, TILE), lambda z, i, l: (0, i[z]))],
        jax.ShapeDtypeStruct((blocks, width, TILE), F32),
        pl.BlockSpec((1, width, TILE), lambda z, i, l: (z, 0, 0)), "pick",
    )
    raw = lax.all_to_all(outgoing, "col", split_axis=0, concat_axis=0, tiled=True)

    part = lax.dynamic_slice(own, (row_tile[col] * TILE, 0), (TILE, depth))
    part = jnp.where(row_ok[col] != 0, part, jnp.zeros_like(part))

    e_here = jnp.logical_and(ie >= 0, ie // td == row)
    e_rows = jnp.concatenate([
        jnp.where(e_here[a], lax.dynamic_slice(own, ((ie[a] % td) * TILE, 0), (TILE, depth)), jnp.zeros((), BF16))
        for a in range(2)
    ])
    e_all = lax.psum(e_rows, ("rx", "core"))
    partner = lax.all_gather(part, ("rx", "core"), axis=0)
    pair_a = jnp.array([0, 0, 1, 1], i32)
    pair_b = jnp.array([0, 1, 0, 1], i32)
    ia, ib, ea, eb = ie[pair_a], ie[pair_b], e[pair_a], e[pair_b]
    live = (ia >= 0) & (ib >= 0) & (pat[jnp.maximum(ia, 0), jnp.maximum(ib, 0)] != 0)
    table = jnp.stack([
        jnp.maximum(ia, 0) % td, jnp.maximum(ib, 0) % td, ea % rd, eb % cd,
        live & (ia // td == row) & (ib // td == col),
        (ea // rd == group) & (eb // cd == col),
        live & (row == 0) & (col == 0),
    ]).astype(i32)
    diag_part = tile_call(
        diag_kernel, (2, 2), (table,), (block, parent_front, e_all, e_all),
        [
            pl.BlockSpec((TILE, TILE), lambda a, b, t: (t[0, a * 2 + b], t[1, a * 2 + b])),
            pl.BlockSpec((TILE, TILE), lambda a, b, t: (t[2, a * 2 + b], t[3, a * 2 + b])),
            pl.BlockSpec((TILE, depth), lambda a, b, t: (a, 0)),
            pl.BlockSpec((TILE, depth), lambda a, b, t: (b, 0)),
        ],
        jax.ShapeDtypeStruct((2 * TILE, 2 * TILE), F32),
        pl.BlockSpec((TILE, TILE), lambda a, b, t: (a, b)), "diag",
    )
    diagonal = lax.psum(diag_part, ("child", "rx", "core", "col"))
    inverse = factor_inverse(diagonal)

    col_ids = jnp.arange(blocks, dtype=i32) * td + in_tile
    factors = pat[row * td + row_tile][:, col_ids] * row_ok[:, None] * in_ok[None, :]
    update = tile_call(
        update_kernel, (chips, blocks), (row_tile, factors), (raw, own, partner),
        [
            pl.BlockSpec((1, TILE, TILE), lambda p, b, r, f: (b, r[p], 0)),
            pl.BlockSpec((TILE, depth), lambda p, b, r, f: (r[p], 0)),
            pl.BlockSpec((1, TILE, depth), lambda p, b, r, f: (b, 0, 0)),
        ],
        jax.ShapeDtypeStruct((chips, TILE, blocks * TILE), F32),
        pl.BlockSpec((1, TILE, TILE), lambda p, b, r, f: (p, 0, b)), "update",
    )
    first = lax.all_to_all(update, ("child", "rx"), split_axis=0, concat_axis=0, tiled=True)
    second = lax.ppermute(first, "core", [(k, (k + 1) % 2) for k in range(2)])

    my_cols = lax.dynamic_slice_in_dim(inv, col * cd, cd, 1)
    my_rows = lax.dynamic_slice_in_dim(inv, group * rd, rd, 1)
    cols_own = lax.dynamic_index_in_dim(my_cols, ci, 0, keepdims=False)
    grid_q = jnp.broadcast_to(jnp.arange(cd, dtype=i32), (2, cd))
    e2 = jnp.broadcast_to(e[:, None], (2, cd))
    cols2 = jnp.broadcast_to(cols_own[None, :], (2, cd))
    table = jnp.stack([
        e2 // cd, jnp.maximum(cols2, 0) // td,
        (e_here[:, None] & (cols2 >= 0)),
        e2 % rd, (e2 // rd == group),
    ]).astype(i32).reshape(5, 2 * cd)
    strip_part = tile_call(
        strip_kernel, (2, cd), (table,), (update, parent_front),
        [
            pl.BlockSpec((1, TILE, TILE), lambda a, q, t: (t[0, a * cd + q], 0, t[1, a * cd + q])),
            pl.BlockSpec((TILE, TILE), lambda a, q, t: (t[3, a * cd + q], q)),
        ],
        jax.ShapeDtypeStruct((2 * TILE, cd * TILE), F32),
        pl.BlockSpec((TILE, TILE), lambda a, q, t: (a, q)), "strip",
    )
    strip = lax.psum(strip_part, ("child", "rx", "core"))
    half = lax.dynamic_slice(strip, (0, core * rd * TILE), (2 * TILE, rd * TILE))
    half = lax.psum(jnp.where(chip == col, half, jnp.zeros_like(half)), "col")
    wc = lax.dot_general(inverse, strip, (((1,), (0,)), ((), ())), precision=lax.Precision.HIGHEST)
    wr = lax.dot_general(inverse, half, (((1,), (0,)), ((), ())), precision=lax.Precision.HIGHEST)

    rr = jnp.broadcast_to(my_rows[:, :, None], (2, rd, cd))
    cc = jnp.broadcast_to(my_cols[:, None, :], (2, rd, cd))
    ok = (rr >= 0) & (cc >= 0)
    send_row = jnp.maximum(rr, 0) // td
    same = send_row % cores == core
    send = jnp.arange(2, dtype=i32)[:, None, None] * rxn + send_row // cores
    from_b = jnp.maximum(cc, 0) // td
    lists = []
    for c in range(2):
        for kind in (same, ~same):
            flag = ok[c] & kind[c]
            lists.append((jnp.where(flag, send[c], 0), jnp.where(flag, from_b[c], 0), flag.astype(i32)))
    here = col * cd + jnp.arange(cd, dtype=i32)
    panel = jnp.where(here == e[0], 1, jnp.where(here == e[1], 2, 0))
    rows = [x[n] for n in (0, 1) for x in lists] + [x[2] for x in lists]
    rows.append(jnp.broadcast_to(panel, (rd, cd)))
    table = jnp.stack(rows).reshape(13, rd * cd)

    def from_list(n):
        return pl.BlockSpec(
            (1, TILE, TILE), lambda i, j, t: (t[n, i * cd + j], 0, t[4 + n, i * cd + j])
        )

    return tile_call(
        final_kernel, (rd, cd), (table,), (parent_front, first, second, first, second, wr, wc),
        [pl.BlockSpec((TILE, TILE), lambda i, j, t: (i, j))] + [from_list(n) for n in range(4)] + [
            pl.BlockSpec((2 * TILE, TILE), lambda i, j, t: (0, i)),
            pl.BlockSpec((2 * TILE, TILE), lambda i, j, t: (0, j)),
        ],
        jax.ShapeDtypeStruct(parent_front.shape, F32),
        pl.BlockSpec((TILE, TILE), lambda i, j, t: (i, j)), "final",
    )


def solution(mesh):
    child, row, col = mesh.devices.shape
    cores = child * row // col
    fine = Mesh(mesh.devices.reshape(child, row // cores, cores, col), ("child", "rx", "core", "col"))
    return jax.shard_map(
        body,
        mesh=fine,
        in_specs=(
            P("child", ("rx", "core"), "col"),
            P("child", ("rx", "core"), None),
            P(),
            P(),
            P(),
            P(("child", "rx", "core"), "col"),
        ),
        out_specs=P(("child", "rx", "core"), "col"),
        check_vma=False,
    )
```

```python
import functools

import jax
import jax.numpy as jnp
from jax import lax
from jax.experimental import pallas as pl
from jax.experimental.pallas import tpu as pltpu
from jax.sharding import Mesh, PartitionSpec as P

TILE = 256
F32 = jnp.float32
BF16 = jnp.bfloat16
NT = (((1,), (1,)), ((), ()))
TN = (((0,), (0,)), ((), ()))


def dot(a, b, dims):
    return lax.dot_general(a, b, dims, preferred_element_type=F32)


def split(x):
    hi = x.astype(BF16)
    return hi, (x - hi.astype(F32)).astype(BF16)


def dot3(a, b, dims):
    ah, al = split(a)
    bh, bl = split(b)
    return dot(ah, bh, dims) + (dot(ah, bl, dims) + dot(al, bh, dims))


def tile_call(kernel, grid, tables, operands, in_specs, out_shape, out_spec, name, cost=None, scratch=()):
    return pl.pallas_call(
        kernel,
        grid_spec=pltpu.PrefetchScalarGridSpec(
            num_scalar_prefetch=len(tables), grid=grid, in_specs=in_specs, out_specs=out_spec,
            scratch_shapes=list(scratch),
        ),
        out_shape=out_shape,
        name=name,
        cost_estimate=cost,
    )(*tables, *operands)


def pick_kernel(idx, loc, src, out):
    ok = loc[pl.program_id(0)] != 0
    out[0] = jnp.where(ok, src[...], jnp.zeros_like(src))


def diag_kernel(t, blk, front, ea, eb, out):
    k = pl.program_id(0) * 2 + pl.program_id(1)
    x = jnp.where(t[4, k] != 0, blk[...], 0.0) + jnp.where(t[5, k] != 0, front[...], 0.0)
    out[...] = x - jnp.where(t[6, k] != 0, dot(ea[...], eb[0], NT), 0.0)


def update_kernel(rows, fac, raw, panel, partner, out):
    f = fac[pl.program_id(0), pl.program_id(1)]
    u = raw[0] - dot(panel[...], partner[0], NT)
    out[0] = jnp.where(f != 0, u, 0.0)


def strip_kernel(t, upd, front, out):
    a, q = pl.program_id(0), pl.program_id(1)
    k = a * pl.num_programs(1) + q
    out[...] = jnp.where(t[2, k] != 0, upd[0], 0.0) + jnp.where(t[4, k] != 0, front[...], 0.0)


def final_kernel(t, front, a0, b0, a1, b1, wr, wc, out):
    k = pl.program_id(0) * pl.num_programs(1) + pl.program_id(1)
    panel = t[12, k]

    @pl.when(panel == 0)
    def _():
        x = front[...]
        for m, src in enumerate((a0, b0, a1, b1)):
            x = x + jnp.where(t[8 + m, k] != 0, src[0], 0.0)
        out[...] = x - dot3(wr[...], wc[...], TN)

    @pl.when(panel == 1)
    def _():
        out[...] = wr[:TILE, :].T

    @pl.when(panel == 2)
    def _():
        out[...] = wr[TILE:, :].T


BASE = 128
FACTOR_WORK = 40_000_000_000
WIDE = 2


def base_inverse(a_ref, d_ref, x_ref):
    n, step = a_ref.shape[0], 8
    ids = lax.broadcasted_iota(jnp.int32, (step, n), 0)
    lanes = lax.broadcasted_iota(jnp.int32, (step, n), 1)
    a = [a_ref[i * step : (i + 1) * step, :] for i in range(n // step)]
    x = [(lanes == ids + i * step).astype(F32) for i in range(n // step)]
    for j in range(0, n, WIDE):
        c0 = j // step
        chunks = range(c0, n // step)
        cols = [[jnp.broadcast_to(a[i][:, j + t : j + t + 1], (step, n)) for i in chunks] for t in range(WIDE)]
        at = [j + t - c0 * step for t in range(WIDE)]
        rows = [a[c0][p : p + 1, :] for p in at]
        xrows = [x[c0][p : p + 1, :] for p in at]
        for t in range(WIDE):
            pivot = cols[t][0][at[t] : at[t] + 1, :]
            d_ref[j + t : j + t + 1, :] = pivot
            inv = 1.0 / pivot
            low = [c * inv for c in cols[t]]
            low[0] = jnp.where(ids > at[t], low[0], 0.0)
            for s in range(t + 1, WIDE):
                f = cols[t][0][at[s] : at[s] + 1, :]
                g = f * inv
                cols[s] = [c - l * f for c, l in zip(cols[s], low)]
                rows[s] = rows[s] - g * rows[t]
                xrows[s] = xrows[s] - g * xrows[t]
            for n_, i in enumerate(chunks):
                a[i] = a[i] - low[n_] * rows[t]
                x[i] = x[i] - low[n_] * xrows[t]
    for i in range(n // step):
        x_ref[i * step : (i + 1) * step, :] = x[i] * (1.0 / jnp.sqrt(d_ref[i * step : (i + 1) * step, :]))


def factor_kernel(a_in, y, a, blk, piv, inv):
    n = a.shape[0]
    high = functools.partial(lax.dot_general, precision=lax.Precision.HIGHEST, preferred_element_type=F32)
    ids = lax.broadcasted_iota(jnp.int32, (n, n), 0)
    a[...] = a_in[...]
    y[...] = (ids == lax.broadcasted_iota(jnp.int32, (n, n), 1)).astype(F32)

    def one(k, carry):
        at = pl.ds(pl.multiple_of(k * BASE, BASE), BASE)
        blk[...] = a[at, at]
        base_inverse(blk, piv, inv)
        low = high(a[:, at], inv[...], NT)
        low = jnp.where(ids[:, :BASE] >= (k + 1) * BASE, low, 0.0)
        yk = high(inv[...], y[at, :], (((1,), (0,)), ((), ())))
        a[...] = a[...] - high(low, low, NT)
        y[...] = y[...] - high(low, yk, (((1,), (0,)), ((), ())))
        y[at, :] = yk
        return carry

    lax.fori_loop(0, n // BASE, one, 0)


def factor_inverse(d):
    n = d.shape[0]
    return pl.pallas_call(
        factor_kernel,
        out_shape=jax.ShapeDtypeStruct(d.shape, F32),
        scratch_shapes=[pltpu.VMEM((n, n), F32)] + [pltpu.VMEM((BASE, BASE), F32)] * 3,
        name="factor",
        cost_estimate=pl.CostEstimate(flops=FACTOR_WORK, bytes_accessed=8 * n * n, transcendentals=0),
    )(d)


def body(child_blocks, child_panels, child_patterns, child_maps, parent_place, parent_front):
    ci = lax.axis_index("child")
    rx = lax.axis_index("rx")
    core = lax.axis_index("core")
    col = lax.axis_index("col")
    cores = lax.axis_size("core")
    rxn = lax.axis_size("rx")
    row = rx * cores + core
    rown = rxn * cores
    chips = lax.axis_size("child") * rxn
    chip = ci * rxn + rx
    group = ci * rown + row
    block = child_blocks[0]
    own = child_panels[0]
    depth = own.shape[1]
    width = block.shape[0]
    td = width // TILE
    blocks = child_maps.shape[1] // td
    rd = parent_front.shape[0] // TILE
    cd = parent_front.shape[1] // TILE
    slots_n = parent_place.shape[0]
    i32 = jnp.int32

    slots = jnp.sum(
        jnp.where(child_maps[:, :, None] == jnp.arange(slots_n, dtype=i32), parent_place, 0), axis=2
    )
    tiles = jnp.arange(child_maps.shape[1], dtype=i32)
    hit = slots[:, None, :] == jnp.arange(slots_n, dtype=i32)[None, :, None]
    inv = jnp.sum(jnp.where(hit, tiles + 1, 0), axis=2) - 1
    mine = lax.dynamic_index_in_dim(slots, ci, 0, keepdims=False).reshape(blocks, td)
    inv_own = lax.dynamic_index_in_dim(inv, ci, 0, keepdims=False)
    pat = lax.dynamic_index_in_dim(child_patterns, ci, 0, keepdims=False)
    m = (mine // cd)[:, None, :] == jnp.arange(chips, dtype=i32)[None, :, None]
    which = jnp.sum(jnp.where(m, jnp.arange(td, dtype=i32), 0), axis=2)
    there = jnp.any(m, axis=2).astype(i32)
    row_tile = lax.dynamic_index_in_dim(which, row, 0, keepdims=False)
    row_ok = lax.dynamic_index_in_dim(there, row, 0, keepdims=False)
    out_tile = lax.dynamic_index_in_dim(which, col, 0, keepdims=False)
    out_ok = lax.dynamic_index_in_dim(there, col, 0, keepdims=False)
    in_tile = lax.dynamic_index_in_dim(which, col, 1, keepdims=False)
    in_ok = lax.dynamic_index_in_dim(there, col, 1, keepdims=False)
    e = parent_place[:2]
    ie = inv_own[e]

    outgoing = tile_call(
        pick_kernel, (blocks,), (out_tile, out_ok), (block,),
        [pl.BlockSpec((width, TILE), lambda z, i, l: (0, i[z]))],
        jax.ShapeDtypeStruct((blocks, width, TILE), F32),
        pl.BlockSpec((1, width, TILE), lambda z, i, l: (z, 0, 0)), "pick",
    )
    raw = lax.all_to_all(outgoing, "col", split_axis=0, concat_axis=0, tiled=True)

    part = lax.dynamic_slice(own, (row_tile[col] * TILE, 0), (TILE, depth))
    part = jnp.where(row_ok[col] != 0, part, jnp.zeros_like(part))

    e_here = jnp.logical_and(ie >= 0, ie // td == row)
    partner = lax.all_gather(part, ("rx", "core"), axis=0)
    pair_a = jnp.array([0, 0, 1, 1], i32)
    pair_b = jnp.array([0, 1, 0, 1], i32)
    ia, ib, ea, eb = ie[pair_a], ie[pair_b], e[pair_a], e[pair_b]
    live = (ia >= 0) & (ib >= 0) & (pat[jnp.maximum(ia, 0), jnp.maximum(ib, 0)] != 0)
    table = jnp.stack([
        jnp.maximum(ia, 0) % td, jnp.maximum(ib, 0) % td, ea % rd, eb % cd,
        live & (ia // td == row) & (ib // td == col),
        (ea // rd == group) & (eb // cd == col),
        live & (ia // td == row) & (eb // cd == col), jnp.maximum(ib, 0) // td,
    ]).astype(i32)
    diag_part = tile_call(
        diag_kernel, (2, 2), (table,), (block, parent_front, own, partner),
        [
            pl.BlockSpec((TILE, TILE), lambda a, b, t: (t[0, a * 2 + b], t[1, a * 2 + b])),
            pl.BlockSpec((TILE, TILE), lambda a, b, t: (t[2, a * 2 + b], t[3, a * 2 + b])),
            pl.BlockSpec((TILE, depth), lambda a, b, t: (t[0, a * 2 + b], 0)),
            pl.BlockSpec((1, TILE, depth), lambda a, b, t: (t[7, a * 2 + b], 0, 0)),
        ],
        jax.ShapeDtypeStruct((2 * TILE, 2 * TILE), F32),
        pl.BlockSpec((TILE, TILE), lambda a, b, t: (a, b)), "diag",
    )
    plane = ("child", "rx", "core")
    diagonal = lax.psum_scatter(diag_part, plane, scatter_dimension=0, tiled=True)
    diagonal = lax.all_gather(lax.psum(diagonal, "col"), plane, axis=0, tiled=True)
    inverse = factor_inverse(diagonal)

    col_ids = jnp.arange(blocks, dtype=i32) * td + in_tile
    factors = pat[row * td + row_tile][:, col_ids] * row_ok[:, None] * in_ok[None, :]
    update = tile_call(
        update_kernel, (chips, blocks), (row_tile, factors), (raw, own, partner),
        [
            pl.BlockSpec((1, TILE, TILE), lambda p, b, r, f: (b, r[p], 0)),
            pl.BlockSpec((TILE, depth), lambda p, b, r, f: (r[p], 0)),
            pl.BlockSpec((1, TILE, depth), lambda p, b, r, f: (b, 0, 0)),
        ],
        jax.ShapeDtypeStruct((chips, TILE, blocks * TILE), F32),
        pl.BlockSpec((1, TILE, TILE), lambda p, b, r, f: (p, 0, b)), "update",
    )
    first = lax.all_to_all(update, ("child", "rx"), split_axis=0, concat_axis=0, tiled=True)
    second = lax.ppermute(first, "core", [(k, (k + 1) % 2) for k in range(2)])

    my_cols = lax.dynamic_slice_in_dim(inv, col * cd, cd, 1)
    my_rows = lax.dynamic_slice_in_dim(inv, group * rd, rd, 1)
    cols_own = lax.dynamic_index_in_dim(my_cols, ci, 0, keepdims=False)
    grid_q = jnp.broadcast_to(jnp.arange(cd, dtype=i32), (2, cd))
    e2 = jnp.broadcast_to(e[:, None], (2, cd))
    cols2 = jnp.broadcast_to(cols_own[None, :], (2, cd))
    table = jnp.stack([
        e2 // cd, jnp.maximum(cols2, 0) // td,
        (e_here[:, None] & (cols2 >= 0)),
        e2 % rd, (e2 // rd == group),
    ]).astype(i32).reshape(5, 2 * cd)
    strip_part = tile_call(
        strip_kernel, (2, cd), (table,), (update, parent_front),
        [
            pl.BlockSpec((1, TILE, TILE), lambda a, q, t: (t[0, a * cd + q], 0, t[1, a * cd + q])),
            pl.BlockSpec((TILE, TILE), lambda a, q, t: (t[3, a * cd + q], q)),
        ],
        jax.ShapeDtypeStruct((2 * TILE, cd * TILE), F32),
        pl.BlockSpec((TILE, TILE), lambda a, q, t: (a, q)), "strip",
    )
    piece = lax.psum_scatter(strip_part, plane, scatter_dimension=0, tiled=True)
    pieces = lax.all_gather(piece, "col", axis=0)
    strip = lax.all_gather(piece, plane, axis=0, tiled=True)
    pieces = pieces.reshape(chips, piece.shape[0], cores, rd * TILE).transpose(0, 2, 1, 3)
    pieces = pieces.reshape(chips * cores, piece.shape[0], rd * TILE)
    half = lax.all_to_all(pieces, plane, split_axis=0, concat_axis=0, tiled=True)
    half = half.reshape(2 * TILE, rd * TILE)
    wc = lax.dot_general(inverse, strip, (((1,), (0,)), ((), ())), precision=lax.Precision.HIGHEST)
    wr = lax.dot_general(inverse, half, (((1,), (0,)), ((), ())), precision=lax.Precision.HIGHEST)

    rr = jnp.broadcast_to(my_rows[:, :, None], (2, rd, cd))
    cc = jnp.broadcast_to(my_cols[:, None, :], (2, rd, cd))
    ok = (rr >= 0) & (cc >= 0)
    send_row = jnp.maximum(rr, 0) // td
    same = send_row % cores == core
    send = jnp.arange(2, dtype=i32)[:, None, None] * rxn + send_row // cores
    from_b = jnp.maximum(cc, 0) // td
    lists = []
    for c in range(2):
        for kind in (same, ~same):
            flag = ok[c] & kind[c]
            lists.append((jnp.where(flag, send[c], 0), jnp.where(flag, from_b[c], 0), flag.astype(i32)))
    here = col * cd + jnp.arange(cd, dtype=i32)
    panel = jnp.where(here == e[0], 1, jnp.where(here == e[1], 2, 0))
    rows = [x[n] for n in (0, 1) for x in lists] + [x[2] for x in lists]
    rows.append(jnp.broadcast_to(panel, (rd, cd)))
    table = jnp.stack(rows).reshape(13, rd * cd)

    def from_list(n):
        return pl.BlockSpec(
            (1, TILE, TILE), lambda i, j, t: (t[n, i * cd + j], 0, t[4 + n, i * cd + j])
        )

    return tile_call(
        final_kernel, (rd, cd), (table,), (parent_front, first, second, first, second, wr, wc),
        [pl.BlockSpec((TILE, TILE), lambda i, j, t: (i, j))] + [from_list(n) for n in range(4)] + [
            pl.BlockSpec((2 * TILE, TILE), lambda i, j, t: (0, i)),
            pl.BlockSpec((2 * TILE, TILE), lambda i, j, t: (0, j)),
        ],
        jax.ShapeDtypeStruct(parent_front.shape, F32),
        pl.BlockSpec((TILE, TILE), lambda i, j, t: (i, j)), "final",
    )


def solution(mesh):
    child, row, col = mesh.devices.shape
    cores = child * row // col
    fine = Mesh(mesh.devices.reshape(child, row // cores, cores, col), ("child", "rx", "core", "col"))
    return jax.shard_map(
        body,
        mesh=fine,
        in_specs=(
            P("child", ("rx", "core"), "col"),
            P("child", ("rx", "core"), None),
            P(),
            P(),
            P(),
            P(("child", "rx", "core"), "col"),
        ),
        out_specs=P(("child", "rx", "core"), "col"),
        check_vma=False,
    )
```

```python
import functools

import jax
import jax.numpy as jnp
from jax import lax
from jax.experimental import pallas as pl
from jax.experimental.pallas import tpu as pltpu
from jax.sharding import Mesh, PartitionSpec as P

TILE = 256
F32 = jnp.float32
BF16 = jnp.bfloat16
META = 16
CODED = TILE + META
FULL = 32767.0
NT = (((1,), (1,)), ((), ()))
TN = (((0,), (0,)), ((), ()))


def dot(a, b, dims):
    return lax.dot_general(a, b, dims, preferred_element_type=F32)


def split(x):
    hi = x.astype(BF16)
    return hi, (x - hi.astype(F32)).astype(BF16)


def dot3(a, b, dims):
    ah, al = split(a)
    bh, bl = split(b)
    return dot(ah, bh, dims) + (dot(ah, bl, dims) + dot(al, bh, dims))


def tile_call(kernel, grid, tables, operands, in_specs, out_shape, out_spec, name, cost=None, scratch=()):
    return pl.pallas_call(
        kernel,
        grid_spec=pltpu.PrefetchScalarGridSpec(
            num_scalar_prefetch=len(tables), grid=grid, in_specs=in_specs, out_specs=out_spec,
            scratch_shapes=list(scratch),
        ),
        out_shape=out_shape,
        name=name,
        cost_estimate=cost,
    )(*tables, *operands)


def powers(k):
    h = jnp.floor(k * 0.5)
    return jnp.exp2(h), jnp.exp2(k - h)


def encode(x):
    top = jnp.maximum(jnp.max(jnp.abs(x), axis=0, keepdims=True), 1e-37)
    k = jnp.ceil(jnp.log2(top) + 1e-3)
    p, r = powers(-k)
    part = jnp.clip(jnp.ceil(top * p * r * FULL), 1.0, FULL)
    q = jnp.clip(x * p * (r * (FULL * FULL / part)), -FULL, FULL)
    q = jnp.floor(q + 0.5).astype(jnp.int32)
    ids = lax.broadcasted_iota(jnp.int32, (META, TILE), 0)
    meta = jnp.where(ids == 0, k.astype(jnp.int32), jnp.where(ids == 1, part.astype(jnp.int32), 0))
    return q.astype(jnp.int16), meta.astype(jnp.int16)


def decode(code):
    meta = code[TILE:, :].astype(jnp.int32).astype(F32)
    p, r = powers(meta[0:1, :])
    q = code[:TILE, :].astype(jnp.int32).astype(F32)
    return q * (meta[1:2, :] * (1.0 / (FULL * FULL)) * p) * r


def pick_kernel(idx, src, out):
    q, meta = encode(src[...])
    out[0, 0, :TILE, :] = q
    out[0, 0, TILE:, :] = meta


def diag_kernel(t, blk, front, ea, eb, out):
    k = pl.program_id(0) * 2 + pl.program_id(1)
    x = jnp.where(t[4, k] != 0, blk[...], 0.0) + jnp.where(t[5, k] != 0, front[...], 0.0)
    out[...] = x - jnp.where(t[6, k] != 0, dot(ea[...], eb[0], NT), 0.0)


def update_kernel(rows, fac, raw, panel, partner, out, coded):
    f = fac[pl.program_id(0), pl.program_id(1)]
    u = decode(raw[0, 0]) - dot(panel[...], partner[0], NT)
    u = jnp.where(f != 0, u, 0.0)
    out[0] = u
    q, meta = encode(u)
    coded[0, :TILE, :] = q
    coded[0, TILE:, :] = meta


def strip_kernel(t, upd, front, out):
    a, q = pl.program_id(0), pl.program_id(1)
    k = a * pl.num_programs(1) + q
    out[...] = jnp.where(t[2, k] != 0, upd[0], 0.0) + jnp.where(t[4, k] != 0, front[...], 0.0)


def final_kernel(t, front, a0, b0, a1, b1, wr, wc, out):
    k = pl.program_id(0) * pl.num_programs(1) + pl.program_id(1)
    panel = t[12, k]

    @pl.when(panel == 0)
    def _():
        out[...] = front[...] - dot3(wr[...], wc[...], TN)
        for m, src in enumerate((a0, b0, a1, b1)):

            @pl.when(t[8 + m, k] != 0)
            def _(src=src):
                out[...] = out[...] + decode(src[0])

    @pl.when(panel == 1)
    def _():
        out[...] = wr[:TILE, :].T

    @pl.when(panel == 2)
    def _():
        out[...] = wr[TILE:, :].T


BASE = 128
FACTOR_WORK = 40_000_000_000
WIDE = 2


def base_inverse(a_ref, d_ref, x_ref):
    n, step = a_ref.shape[0], 8
    ids = lax.broadcasted_iota(jnp.int32, (step, n), 0)
    lanes = lax.broadcasted_iota(jnp.int32, (step, n), 1)
    a = [a_ref[i * step : (i + 1) * step, :] for i in range(n // step)]
    x = [(lanes == ids + i * step).astype(F32) for i in range(n // step)]
    for j in range(0, n, WIDE):
        c0 = j // step
        chunks = range(c0, n // step)
        cols = [[jnp.broadcast_to(a[i][:, j + t : j + t + 1], (step, n)) for i in chunks] for t in range(WIDE)]
        at = [j + t - c0 * step for t in range(WIDE)]
        rows = [a[c0][p : p + 1, :] for p in at]
        xrows = [x[c0][p : p + 1, :] for p in at]
        for t in range(WIDE):
            pivot = cols[t][0][at[t] : at[t] + 1, :]
            d_ref[j + t : j + t + 1, :] = pivot
            inv = 1.0 / pivot
            low = [c * inv for c in cols[t]]
            low[0] = jnp.where(ids > at[t], low[0], 0.0)
            for s in range(t + 1, WIDE):
                f = cols[t][0][at[s] : at[s] + 1, :]
                g = f * inv
                cols[s] = [c - l * f for c, l in zip(cols[s], low)]
                rows[s] = rows[s] - g * rows[t]
                xrows[s] = xrows[s] - g * xrows[t]
            for n_, i in enumerate(chunks):
                a[i] = a[i] - low[n_] * rows[t]
                x[i] = x[i] - low[n_] * xrows[t]
    for i in range(n // step):
        x_ref[i * step : (i + 1) * step, :] = x[i] * (1.0 / jnp.sqrt(d_ref[i * step : (i + 1) * step, :]))


def factor_kernel(a_in, y, a, blk, piv, inv):
    n = a.shape[0]
    high = functools.partial(lax.dot_general, precision=lax.Precision.HIGHEST, preferred_element_type=F32)
    ids = lax.broadcasted_iota(jnp.int32, (n, n), 0)
    a[...] = a_in[...]
    y[...] = (ids == lax.broadcasted_iota(jnp.int32, (n, n), 1)).astype(F32)

    def one(k, carry):
        at = pl.ds(pl.multiple_of(k * BASE, BASE), BASE)
        blk[...] = a[at, at]
        base_inverse(blk, piv, inv)
        low = high(a[:, at], inv[...], NT)
        low = jnp.where(ids[:, :BASE] >= (k + 1) * BASE, low, 0.0)
        yk = high(inv[...], y[at, :], (((1,), (0,)), ((), ())))
        a[...] = a[...] - high(low, low, NT)
        y[...] = y[...] - high(low, yk, (((1,), (0,)), ((), ())))
        y[at, :] = yk
        return carry

    lax.fori_loop(0, n // BASE, one, 0)


def factor_inverse(d):
    n = d.shape[0]
    return pl.pallas_call(
        factor_kernel,
        out_shape=jax.ShapeDtypeStruct(d.shape, F32),
        scratch_shapes=[pltpu.VMEM((n, n), F32)] + [pltpu.VMEM((BASE, BASE), F32)] * 3,
        name="factor",
        cost_estimate=pl.CostEstimate(flops=FACTOR_WORK, bytes_accessed=8 * n * n, transcendentals=0),
    )(d)


def body(child_blocks, child_panels, child_patterns, child_maps, parent_place, parent_front):
    ci = lax.axis_index("child")
    rx = lax.axis_index("rx")
    core = lax.axis_index("core")
    col = lax.axis_index("col")
    cores = lax.axis_size("core")
    rxn = lax.axis_size("rx")
    row = rx * cores + core
    rown = rxn * cores
    chips = lax.axis_size("child") * rxn
    chip = ci * rxn + rx
    group = ci * rown + row
    block = child_blocks[0]
    own = child_panels[0]
    depth = own.shape[1]
    width = block.shape[0]
    td = width // TILE
    blocks = child_maps.shape[1] // td
    rd = parent_front.shape[0] // TILE
    cd = parent_front.shape[1] // TILE
    slots_n = parent_place.shape[0]
    i32 = jnp.int32

    slots = jnp.sum(
        jnp.where(child_maps[:, :, None] == jnp.arange(slots_n, dtype=i32), parent_place, 0), axis=2
    )
    tiles = jnp.arange(child_maps.shape[1], dtype=i32)
    hit = slots[:, None, :] == jnp.arange(slots_n, dtype=i32)[None, :, None]
    inv = jnp.sum(jnp.where(hit, tiles + 1, 0), axis=2) - 1
    mine = lax.dynamic_index_in_dim(slots, ci, 0, keepdims=False).reshape(blocks, td)
    inv_own = lax.dynamic_index_in_dim(inv, ci, 0, keepdims=False)
    pat = lax.dynamic_index_in_dim(child_patterns, ci, 0, keepdims=False)
    m = (mine // cd)[:, None, :] == jnp.arange(chips, dtype=i32)[None, :, None]
    which = jnp.sum(jnp.where(m, jnp.arange(td, dtype=i32), 0), axis=2)
    there = jnp.any(m, axis=2).astype(i32)
    row_tile = lax.dynamic_index_in_dim(which, row, 0, keepdims=False)
    row_ok = lax.dynamic_index_in_dim(there, row, 0, keepdims=False)
    out_tile = lax.dynamic_index_in_dim(which, col, 0, keepdims=False)
    in_tile = lax.dynamic_index_in_dim(which, col, 1, keepdims=False)
    in_ok = lax.dynamic_index_in_dim(there, col, 1, keepdims=False)
    e = parent_place[:2]
    ie = inv_own[e]

    outgoing = tile_call(
        pick_kernel, (blocks, td), (out_tile,), (block,),
        [pl.BlockSpec((TILE, TILE), lambda z, r, i: (r, i[z]))],
        jax.ShapeDtypeStruct((blocks, td, CODED, TILE), jnp.int16),
        pl.BlockSpec((1, 1, CODED, TILE), lambda z, r, i: (z, r, 0, 0)), "pick",
    )
    raw = lax.all_to_all(outgoing, "col", split_axis=0, concat_axis=0, tiled=True)

    part = lax.dynamic_slice(own, (row_tile[col] * TILE, 0), (TILE, depth))
    part = jnp.where(row_ok[col] != 0, part, jnp.zeros_like(part))

    e_here = jnp.logical_and(ie >= 0, ie // td == row)
    partner = lax.all_gather(part, ("rx", "core"), axis=0)
    pair_a = jnp.array([0, 0, 1, 1], i32)
    pair_b = jnp.array([0, 1, 0, 1], i32)
    ia, ib, ea, eb = ie[pair_a], ie[pair_b], e[pair_a], e[pair_b]
    live = (ia >= 0) & (ib >= 0) & (pat[jnp.maximum(ia, 0), jnp.maximum(ib, 0)] != 0)
    table = jnp.stack([
        jnp.maximum(ia, 0) % td, jnp.maximum(ib, 0) % td, ea % rd, eb % cd,
        live & (ia // td == row) & (ib // td == col),
        (ea // rd == group) & (eb // cd == col),
        live & (ia // td == row) & (eb // cd == col), jnp.maximum(ib, 0) // td,
    ]).astype(i32)
    diag_part = tile_call(
        diag_kernel, (2, 2), (table,), (block, parent_front, own, partner),
        [
            pl.BlockSpec((TILE, TILE), lambda a, b, t: (t[0, a * 2 + b], t[1, a * 2 + b])),
            pl.BlockSpec((TILE, TILE), lambda a, b, t: (t[2, a * 2 + b], t[3, a * 2 + b])),
            pl.BlockSpec((TILE, depth), lambda a, b, t: (t[0, a * 2 + b], 0)),
            pl.BlockSpec((1, TILE, depth), lambda a, b, t: (t[7, a * 2 + b], 0, 0)),
        ],
        jax.ShapeDtypeStruct((2 * TILE, 2 * TILE), F32),
        pl.BlockSpec((TILE, TILE), lambda a, b, t: (a, b)), "diag",
    )
    plane = ("child", "rx", "core")
    every = ("child", "rx", "core", "col")
    devices = lax.axis_size(every)
    diagonal = diag_part.reshape(devices, 2 * TILE // devices, 2 * TILE)
    diagonal = lax.all_to_all(diagonal, every, split_axis=0, concat_axis=0, tiled=True)
    diagonal, partner = lax.optimization_barrier((jnp.sum(diagonal, axis=0), partner))
    diagonal = lax.all_gather(diagonal, every, axis=0, tiled=True)
    inverse = factor_inverse(diagonal)

    col_ids = jnp.arange(blocks, dtype=i32) * td + in_tile
    factors = pat[row * td + row_tile][:, col_ids] * row_ok[:, None] * in_ok[None, :]
    update, coded = tile_call(
        update_kernel, (chips, blocks), (row_tile, factors), (raw, own, partner),
        [
            pl.BlockSpec((1, 1, CODED, TILE), lambda p, b, r, f: (b, r[p], 0, 0)),
            pl.BlockSpec((TILE, depth), lambda p, b, r, f: (r[p], 0)),
            pl.BlockSpec((1, TILE, depth), lambda p, b, r, f: (b, 0, 0)),
        ],
        [
            jax.ShapeDtypeStruct((chips, TILE, blocks * TILE), F32),
            jax.ShapeDtypeStruct((chips, CODED, blocks * TILE), jnp.int16),
        ],
        [
            pl.BlockSpec((1, TILE, TILE), lambda p, b, r, f: (p, 0, b)),
            pl.BlockSpec((1, CODED, TILE), lambda p, b, r, f: (p, 0, b)),
        ], "update",
    )
    first = lax.all_to_all(coded, ("child", "rx"), split_axis=0, concat_axis=0, tiled=True)
    second = lax.ppermute(first, "core", [(k, (k + 1) % 2) for k in range(2)])

    my_cols = lax.dynamic_slice_in_dim(inv, col * cd, cd, 1)
    my_rows = lax.dynamic_slice_in_dim(inv, group * rd, rd, 1)
    cols_own = lax.dynamic_index_in_dim(my_cols, ci, 0, keepdims=False)
    grid_q = jnp.broadcast_to(jnp.arange(cd, dtype=i32), (2, cd))
    e2 = jnp.broadcast_to(e[:, None], (2, cd))
    cols2 = jnp.broadcast_to(cols_own[None, :], (2, cd))
    table = jnp.stack([
        e2 // cd, jnp.maximum(cols2, 0) // td,
        (e_here[:, None] & (cols2 >= 0)),
        e2 % rd, (e2 // rd == group),
    ]).astype(i32).reshape(5, 2 * cd)
    strip_part = tile_call(
        strip_kernel, (2, cd), (table,), (update, parent_front),
        [
            pl.BlockSpec((1, TILE, TILE), lambda a, q, t: (t[0, a * cd + q], 0, t[1, a * cd + q])),
            pl.BlockSpec((TILE, TILE), lambda a, q, t: (t[3, a * cd + q], q)),
        ],
        jax.ShapeDtypeStruct((2 * TILE, cd * TILE), F32),
        pl.BlockSpec((TILE, TILE), lambda a, q, t: (a, q)), "strip",
    )
    piece = lax.psum_scatter(strip_part, plane, scatter_dimension=0, tiled=True)
    pieces = lax.all_gather(piece, "col", axis=0)
    strip = lax.all_gather(piece, plane, axis=0, tiled=True)
    pieces = pieces.reshape(chips, piece.shape[0], cores, rd * TILE).transpose(0, 2, 1, 3)
    pieces = pieces.reshape(chips * cores, piece.shape[0], rd * TILE)
    half = lax.all_to_all(pieces, plane, split_axis=0, concat_axis=0, tiled=True)
    half = half.reshape(2 * TILE, rd * TILE)
    wc = lax.dot_general(inverse, strip, (((1,), (0,)), ((), ())), precision=lax.Precision.HIGHEST)
    wr = lax.dot_general(inverse, half, (((1,), (0,)), ((), ())), precision=lax.Precision.HIGHEST)

    rr = jnp.broadcast_to(my_rows[:, :, None], (2, rd, cd))
    cc = jnp.broadcast_to(my_cols[:, None, :], (2, rd, cd))
    ok = (rr >= 0) & (cc >= 0)
    send_row = jnp.maximum(rr, 0) // td
    same = send_row % cores == core
    send = jnp.arange(2, dtype=i32)[:, None, None] * rxn + send_row // cores
    from_b = jnp.maximum(cc, 0) // td
    lists = []
    for c in range(2):
        for kind in (same, ~same):
            flag = ok[c] & kind[c]
            lists.append((jnp.where(flag, send[c], 0), jnp.where(flag, from_b[c], 0), flag.astype(i32)))
    here = col * cd + jnp.arange(cd, dtype=i32)
    panel = jnp.where(here == e[0], 1, jnp.where(here == e[1], 2, 0))
    rows = [x[n] for n in (0, 1) for x in lists] + [x[2] for x in lists]
    rows.append(jnp.broadcast_to(panel, (rd, cd)))
    table = jnp.stack(rows).reshape(13, rd * cd)

    def from_list(n):
        return pl.BlockSpec(
            (1, CODED, TILE), lambda i, j, t: (t[n, i * cd + j], 0, t[4 + n, i * cd + j])
        )

    return tile_call(
        final_kernel, (rd, cd), (table,), (parent_front, first, second, first, second, wr, wc),
        [pl.BlockSpec((TILE, TILE), lambda i, j, t: (i, j))] + [from_list(n) for n in range(4)] + [
            pl.BlockSpec((2 * TILE, TILE), lambda i, j, t: (0, i)),
            pl.BlockSpec((2 * TILE, TILE), lambda i, j, t: (0, j)),
        ],
        jax.ShapeDtypeStruct(parent_front.shape, F32),
        pl.BlockSpec((TILE, TILE), lambda i, j, t: (i, j)), "final",
    )


def solution(mesh):
    child, row, col = mesh.devices.shape
    cores = child * row // col
    fine = Mesh(mesh.devices.reshape(child, row // cores, cores, col), ("child", "rx", "core", "col"))
    return jax.shard_map(
        body,
        mesh=fine,
        in_specs=(
            P("child", ("rx", "core"), "col"),
            P("child", ("rx", "core"), None),
            P(),
            P(),
            P(),
            P(("child", "rx", "core"), "col"),
        ),
        out_specs=P(("child", "rx", "core"), "col"),
        check_vma=False,
    )
```

```python
import functools

import jax
import jax.numpy as jnp
from jax import lax
from jax.experimental import pallas as pl
from jax.experimental.pallas import tpu as pltpu
from jax.sharding import Mesh, PartitionSpec as P

TILE = 256
F32 = jnp.float32
BF16 = jnp.bfloat16
META = 16
CODED = TILE + META
FULL = 32767.0
NT = (((1,), (1,)), ((), ()))
NN = (((1,), (0,)), ((), ()))


def dot(a, b, dims):
    return lax.dot_general(a, b, dims, preferred_element_type=F32)


def split(x):
    hi = x.astype(BF16)
    return hi, (x - hi.astype(F32)).astype(BF16)


def tile_call(kernel, grid, tables, operands, in_specs, out_shape, out_spec, name, cost=None, scratch=()):
    return pl.pallas_call(
        kernel,
        grid_spec=pltpu.PrefetchScalarGridSpec(
            num_scalar_prefetch=len(tables), grid=grid, in_specs=in_specs, out_specs=out_spec,
            scratch_shapes=list(scratch),
        ),
        out_shape=out_shape,
        name=name,
        cost_estimate=cost,
    )(*tables, *operands)


def powers(k):
    h = jnp.floor(k * 0.5)
    return jnp.exp2(h), jnp.exp2(k - h)


def encode(x):
    top = jnp.maximum(jnp.max(jnp.abs(x), axis=0, keepdims=True), 1e-37)
    k = jnp.ceil(jnp.log2(top) + 1e-3)
    p, r = powers(-k)
    part = jnp.clip(jnp.ceil(top * p * r * FULL), 1.0, FULL)
    q = jnp.clip(x * p * (r * (FULL * FULL / part)), -FULL, FULL)
    q = jnp.floor(q + 0.5).astype(jnp.int32)
    ids = lax.broadcasted_iota(jnp.int32, (META, TILE), 0)
    meta = jnp.where(ids == 0, k.astype(jnp.int32), jnp.where(ids == 1, part.astype(jnp.int32), 0))
    return q.astype(jnp.int16), meta.astype(jnp.int16)


def decode(code):
    meta = code[TILE:, :].astype(jnp.int32).astype(F32)
    p, r = powers(meta[0:1, :])
    q = code[:TILE, :].astype(jnp.int32).astype(F32)
    return q * (meta[1:2, :] * (1.0 / (FULL * FULL)) * p) * r


def pick_kernel(idx, src, out):
    q, meta = encode(src[...])
    out[0, 0, :TILE, :] = q
    out[0, 0, TILE:, :] = meta


def diag_kernel(t, blk, front, ea, eb, out):
    k = pl.program_id(0) * 2 + pl.program_id(1)
    x = jnp.where(t[4, k] != 0, blk[...], 0.0) + jnp.where(t[5, k] != 0, front[...], 0.0)
    out[...] = x - jnp.where(t[6, k] != 0, dot(ea[...], eb[0], NT), 0.0)


def update_kernel(rows, fac, raw, panel, partner, out, coded):
    f = fac[pl.program_id(0), pl.program_id(1)]
    u = decode(raw[0, 0]) - dot(panel[...], partner[0], NT)
    u = jnp.where(f != 0, u, 0.0)
    out[0] = u
    q, meta = encode(u)
    coded[0, :TILE, :] = q
    coded[0, TILE:, :] = meta


def strip_kernel(t, upd, front, out):
    a, q = pl.program_id(0), pl.program_id(1)
    k = a * pl.num_programs(1) + q
    out[...] = jnp.where(t[2, k] != 0, upd[0], 0.0) + jnp.where(t[4, k] != 0, front[...], 0.0)


def final_kernel(t, front, a0, b0, a1, b1, wr, wc, out, wrh, wrl):
    k = pl.program_id(0) * pl.num_programs(1) + pl.program_id(1)
    panel = t[12, k]

    @pl.when(pl.program_id(1) == 0)
    def _():
        wrh[...], wrl[...] = split(wr[...])

    @pl.when(panel == 0)
    def _():
        wch, wcl = split(wc[...])
        big = dot(wrh[...], wch, NN)
        out[...] = front[...] - (big + (dot(wrh[...], wcl, NN) + dot(wrl[...], wch, NN)))
        for m, src in enumerate((a0, b0, a1, b1)):

            @pl.when(t[8 + m, k] != 0)
            def _(src=src):
                out[...] = out[...] + decode(src[0])

    @pl.when(panel == 1)
    def _():
        out[...] = wr[:, :TILE]

    @pl.when(panel == 2)
    def _():
        out[...] = wr[:, TILE:]


BASE = 128
FACTOR_WORK = 40_000_000_000
WIDE = 2


def base_inverse(a_ref, d_ref, x_ref):
    n, step = a_ref.shape[0], 8
    ids = lax.broadcasted_iota(jnp.int32, (step, n), 0)
    lanes = lax.broadcasted_iota(jnp.int32, (step, n), 1)
    a = [a_ref[i * step : (i + 1) * step, :] for i in range(n // step)]
    x = [(lanes == ids + i * step).astype(F32) for i in range(n // step)]
    for j in range(0, n, WIDE):
        c0 = j // step
        chunks = range(c0, n // step)
        cols = [[jnp.broadcast_to(a[i][:, j + t : j + t + 1], (step, n)) for i in chunks] for t in range(WIDE)]
        at = [j + t - c0 * step for t in range(WIDE)]
        rows = [a[c0][p : p + 1, :] for p in at]
        xrows = [x[c0][p : p + 1, :] for p in at]
        for t in range(WIDE):
            pivot = cols[t][0][at[t] : at[t] + 1, :]
            d_ref[j + t : j + t + 1, :] = pivot
            inv = 1.0 / pivot
            low = [c * inv for c in cols[t]]
            low[0] = jnp.where(ids > at[t], low[0], 0.0)
            for s in range(t + 1, WIDE):
                f = cols[t][0][at[s] : at[s] + 1, :]
                g = f * inv
                cols[s] = [c - l * f for c, l in zip(cols[s], low)]
                rows[s] = rows[s] - g * rows[t]
                xrows[s] = xrows[s] - g * xrows[t]
            for n_, i in enumerate(chunks):
                a[i] = a[i] - low[n_] * rows[t]
                x[i] = x[i] - low[n_] * xrows[t]
    for i in range(n // step):
        x_ref[i * step : (i + 1) * step, :] = x[i] * (1.0 / jnp.sqrt(d_ref[i * step : (i + 1) * step, :]))


def factor_kernel(a_in, y, a, blk, piv, inv):
    n = a.shape[0]
    high = functools.partial(lax.dot_general, precision=lax.Precision.HIGHEST, preferred_element_type=F32)
    ids = lax.broadcasted_iota(jnp.int32, (n, n), 0)
    a[...] = a_in[...]
    y[...] = (ids == lax.broadcasted_iota(jnp.int32, (n, n), 1)).astype(F32)

    def one(k, carry):
        at = pl.ds(pl.multiple_of(k * BASE, BASE), BASE)
        blk[...] = a[at, at]
        base_inverse(blk, piv, inv)
        low = high(a[:, at], inv[...], NT)
        low = jnp.where(ids[:, :BASE] >= (k + 1) * BASE, low, 0.0)
        yk = high(inv[...], y[at, :], (((1,), (0,)), ((), ())))
        a[...] = a[...] - high(low, low, NT)
        y[...] = y[...] - high(low, yk, (((1,), (0,)), ((), ())))
        y[at, :] = yk
        return carry

    lax.fori_loop(0, n // BASE, one, 0)


def factor_inverse(d):
    n = d.shape[0]
    return pl.pallas_call(
        factor_kernel,
        out_shape=jax.ShapeDtypeStruct(d.shape, F32),
        scratch_shapes=[pltpu.VMEM((n, n), F32)] + [pltpu.VMEM((BASE, BASE), F32)] * 3,
        name="factor",
        cost_estimate=pl.CostEstimate(flops=FACTOR_WORK, bytes_accessed=8 * n * n, transcendentals=0),
    )(d)


def body(child_blocks, child_panels, child_patterns, child_maps, parent_place, parent_front):
    ci = lax.axis_index("child")
    rx = lax.axis_index("rx")
    core = lax.axis_index("core")
    col = lax.axis_index("col")
    cores = lax.axis_size("core")
    rxn = lax.axis_size("rx")
    row = rx * cores + core
    rown = rxn * cores
    chips = lax.axis_size("child") * rxn
    chip = ci * rxn + rx
    group = ci * rown + row
    block = child_blocks[0]
    own = child_panels[0]
    depth = own.shape[1]
    width = block.shape[0]
    td = width // TILE
    blocks = child_maps.shape[1] // td
    rd = parent_front.shape[0] // TILE
    cd = parent_front.shape[1] // TILE
    slots_n = parent_place.shape[0]
    i32 = jnp.int32

    slots = jnp.sum(
        jnp.where(child_maps[:, :, None] == jnp.arange(slots_n, dtype=i32), parent_place, 0), axis=2
    )
    tiles = jnp.arange(child_maps.shape[1], dtype=i32)
    hit = slots[:, None, :] == jnp.arange(slots_n, dtype=i32)[None, :, None]
    inv = jnp.sum(jnp.where(hit, tiles + 1, 0), axis=2) - 1
    mine = lax.dynamic_index_in_dim(slots, ci, 0, keepdims=False).reshape(blocks, td)
    inv_own = lax.dynamic_index_in_dim(inv, ci, 0, keepdims=False)
    pat = lax.dynamic_index_in_dim(child_patterns, ci, 0, keepdims=False)
    m = (mine // cd)[:, None, :] == jnp.arange(chips, dtype=i32)[None, :, None]
    which = jnp.sum(jnp.where(m, jnp.arange(td, dtype=i32), 0), axis=2)
    there = jnp.any(m, axis=2).astype(i32)
    row_tile = lax.dynamic_index_in_dim(which, row, 0, keepdims=False)
    row_ok = lax.dynamic_index_in_dim(there, row, 0, keepdims=False)
    out_tile = lax.dynamic_index_in_dim(which, col, 0, keepdims=False)
    in_tile = lax.dynamic_index_in_dim(which, col, 1, keepdims=False)
    in_ok = lax.dynamic_index_in_dim(there, col, 1, keepdims=False)
    e = parent_place[:2]
    ie = inv_own[e]

    outgoing = tile_call(
        pick_kernel, (blocks, td), (out_tile,), (block,),
        [pl.BlockSpec((TILE, TILE), lambda z, r, i: (r, i[z]))],
        jax.ShapeDtypeStruct((blocks, td, CODED, TILE), jnp.int16),
        pl.BlockSpec((1, 1, CODED, TILE), lambda z, r, i: (z, r, 0, 0)), "pick",
    )
    raw = lax.all_to_all(outgoing, "col", split_axis=0, concat_axis=0, tiled=True)

    part = lax.dynamic_slice(own, (row_tile[col] * TILE, 0), (TILE, depth))
    part = jnp.where(row_ok[col] != 0, part, jnp.zeros_like(part))

    e_here = jnp.logical_and(ie >= 0, ie // td == row)
    partner = lax.all_gather(part, ("rx", "core"), axis=0)
    pair_a = jnp.array([0, 0, 1, 1], i32)
    pair_b = jnp.array([0, 1, 0, 1], i32)
    ia, ib, ea, eb = ie[pair_a], ie[pair_b], e[pair_a], e[pair_b]
    live = (ia >= 0) & (ib >= 0) & (pat[jnp.maximum(ia, 0), jnp.maximum(ib, 0)] != 0)
    table = jnp.stack([
        jnp.maximum(ia, 0) % td, jnp.maximum(ib, 0) % td, ea % rd, eb % cd,
        live & (ia // td == row) & (ib // td == col),
        (ea // rd == group) & (eb // cd == col),
        live & (ia // td == row) & (eb // cd == col), jnp.maximum(ib, 0) // td,
    ]).astype(i32)
    diag_part = tile_call(
        diag_kernel, (2, 2), (table,), (block, parent_front, own, partner),
        [
            pl.BlockSpec((TILE, TILE), lambda a, b, t: (t[0, a * 2 + b], t[1, a * 2 + b])),
            pl.BlockSpec((TILE, TILE), lambda a, b, t: (t[2, a * 2 + b], t[3, a * 2 + b])),
            pl.BlockSpec((TILE, depth), lambda a, b, t: (t[0, a * 2 + b], 0)),
            pl.BlockSpec((1, TILE, depth), lambda a, b, t: (t[7, a * 2 + b], 0, 0)),
        ],
        jax.ShapeDtypeStruct((2 * TILE, 2 * TILE), F32),
        pl.BlockSpec((TILE, TILE), lambda a, b, t: (a, b)), "diag",
    )
    plane = ("child", "rx", "core")
    every = ("child", "rx", "core", "col")
    devices = lax.axis_size(every)
    diagonal = diag_part.reshape(devices, 2 * TILE // devices, 2 * TILE)
    diagonal = lax.all_to_all(diagonal, every, split_axis=0, concat_axis=0, tiled=True)
    diagonal = lax.all_gather(jnp.sum(diagonal, axis=0), every, axis=0, tiled=True)
    diagonal, partner = lax.optimization_barrier((diagonal, partner))
    inverse = factor_inverse(diagonal)

    col_ids = jnp.arange(blocks, dtype=i32) * td + in_tile
    factors = pat[row * td + row_tile][:, col_ids] * row_ok[:, None] * in_ok[None, :]
    update, coded = tile_call(
        update_kernel, (chips, blocks), (row_tile, factors), (raw, own, partner),
        [
            pl.BlockSpec((1, 1, CODED, TILE), lambda p, b, r, f: (b, r[p], 0, 0)),
            pl.BlockSpec((TILE, depth), lambda p, b, r, f: (r[p], 0)),
            pl.BlockSpec((1, TILE, depth), lambda p, b, r, f: (b, 0, 0)),
        ],
        [
            jax.ShapeDtypeStruct((chips, TILE, blocks * TILE), F32),
            jax.ShapeDtypeStruct((chips, CODED, blocks * TILE), jnp.int16),
        ],
        [
            pl.BlockSpec((1, TILE, TILE), lambda p, b, r, f: (p, 0, b)),
            pl.BlockSpec((1, CODED, TILE), lambda p, b, r, f: (p, 0, b)),
        ], "update",
    )
    first = lax.all_to_all(coded, ("child", "rx"), split_axis=0, concat_axis=0, tiled=True)
    second = lax.ppermute(first, "core", [(k, (k + 1) % 2) for k in range(2)])

    my_cols = lax.dynamic_slice_in_dim(inv, col * cd, cd, 1)
    my_rows = lax.dynamic_slice_in_dim(inv, group * rd, rd, 1)
    cols_own = lax.dynamic_index_in_dim(my_cols, ci, 0, keepdims=False)
    grid_q = jnp.broadcast_to(jnp.arange(cd, dtype=i32), (2, cd))
    e2 = jnp.broadcast_to(e[:, None], (2, cd))
    cols2 = jnp.broadcast_to(cols_own[None, :], (2, cd))
    table = jnp.stack([
        e2 // cd, jnp.maximum(cols2, 0) // td,
        (e_here[:, None] & (cols2 >= 0)),
        e2 % rd, (e2 // rd == group),
    ]).astype(i32).reshape(5, 2 * cd)
    strip_part = tile_call(
        strip_kernel, (2, cd), (table,), (update, parent_front),
        [
            pl.BlockSpec((1, TILE, TILE), lambda a, q, t: (t[0, a * cd + q], 0, t[1, a * cd + q])),
            pl.BlockSpec((TILE, TILE), lambda a, q, t: (t[3, a * cd + q], q)),
        ],
        jax.ShapeDtypeStruct((2 * TILE, cd * TILE), F32),
        pl.BlockSpec((TILE, TILE), lambda a, q, t: (a, q)), "strip",
    )
    piece = lax.psum_scatter(strip_part, plane, scatter_dimension=0, tiled=True)
    pieces = jnp.broadcast_to(piece[None], (blocks,) + piece.shape)
    pieces = lax.all_to_all(pieces, "col", split_axis=0, concat_axis=0, tiled=True)
    strip = lax.all_gather(piece, plane, axis=0, tiled=True)
    pieces = pieces.reshape(chips, piece.shape[0], cores, rd * TILE).transpose(0, 2, 1, 3)
    pieces = pieces.reshape(chips * cores, piece.shape[0], rd * TILE)
    half = lax.all_to_all(pieces, plane, split_axis=0, concat_axis=0, tiled=True)
    half = half.reshape(2 * TILE, rd * TILE)
    wc = lax.dot_general(inverse, strip, (((1,), (0,)), ((), ())), precision=lax.Precision.HIGHEST)
    wr = lax.dot_general(half, inverse, (((0,), (1,)), ((), ())), precision=lax.Precision.HIGHEST)

    rr = jnp.broadcast_to(my_rows[:, :, None], (2, rd, cd))
    cc = jnp.broadcast_to(my_cols[:, None, :], (2, rd, cd))
    ok = (rr >= 0) & (cc >= 0)
    send_row = jnp.maximum(rr, 0) // td
    same = send_row % cores == core
    send = jnp.arange(2, dtype=i32)[:, None, None] * rxn + send_row // cores
    from_b = jnp.maximum(cc, 0) // td
    lists = []
    for c in range(2):
        for kind in (same, ~same):
            flag = ok[c] & kind[c]
            lists.append((jnp.where(flag, send[c], 0), jnp.where(flag, from_b[c], 0), flag.astype(i32)))
    here = col * cd + jnp.arange(cd, dtype=i32)
    panel = jnp.where(here == e[0], 1, jnp.where(here == e[1], 2, 0))
    rows = [x[n] for n in (0, 1) for x in lists] + [x[2] for x in lists]
    rows.append(jnp.broadcast_to(panel, (rd, cd)))
    table = jnp.stack(rows).reshape(13, rd * cd)

    def from_list(n):
        return pl.BlockSpec(
            (1, CODED, TILE), lambda i, j, t: (t[n, i * cd + j], 0, t[4 + n, i * cd + j])
        )

    return tile_call(
        final_kernel, (rd, cd), (table,), (parent_front, first, second, first, second, wr, wc),
        [pl.BlockSpec((TILE, TILE), lambda i, j, t: (i, j))] + [from_list(n) for n in range(4)] + [
            pl.BlockSpec((TILE, 2 * TILE), lambda i, j, t: (i, 0)),
            pl.BlockSpec((2 * TILE, TILE), lambda i, j, t: (0, j)),
        ],
        jax.ShapeDtypeStruct(parent_front.shape, F32),
        pl.BlockSpec((TILE, TILE), lambda i, j, t: (i, j)), "final",
        scratch=[pltpu.VMEM((TILE, 2 * TILE), BF16)] * 2,
    )


def solution(mesh):
    child, row, col = mesh.devices.shape
    cores = child * row // col
    fine = Mesh(mesh.devices.reshape(child, row // cores, cores, col), ("child", "rx", "core", "col"))
    return jax.shard_map(
        body,
        mesh=fine,
        in_specs=(
            P("child", ("rx", "core"), "col"),
            P("child", ("rx", "core"), None),
            P(),
            P(),
            P(),
            P(("child", "rx", "core"), "col"),
        ),
        out_specs=P(("child", "rx", "core"), "col"),
        check_vma=False,
    )
```
